32 devices in a mesh: dp: 4 (over y, x), ctx: 8 (over z, core).
Axes of the slice: x: 2, y: 2, z: 4, core: 2. Of those that a mesh axis runs over, the one named last changes fastest.
Arguments:
- block_input: float32 [4, 1024, 768], P('dp', 'ctx'), may hold values from -6 to 6
- out_cotangent: float32 [4, 1024, 768], P('dp', 'ctx'), may hold values from -6 to 6
- first_gain: float32 [768], replicated, may hold values from 0.25 to 1.75
- first_shift: float32 [768], replicated, may hold values from -3 to 3
- mix_weight: bfloat16 [768, 2304], P('dp'), may hold values from -0.21875 to 0.21875
- query_bias: float32 [768], replicated, may hold values from -3 to 3
- value_bias: float32 [768], replicated, may hold values from -3 to 3
- attn_weight: bfloat16 [768, 768], P('dp'), may hold values from -0.75 to 0.75
- attn_bias: float32 [768], replicated, may hold values from -3 to 3
- second_gain: float32 [768], replicated, may hold values from 0.25 to 1.75
- second_shift: float32 [768], replicated, may hold values from -3 to 3
- up_weight: bfloat16 [768, 3072], P('dp'), may hold values from -0.21875 to 0.21875
- up_bias: float32 [3072], replicated, may hold values from -3 to 3
- down_weight: bfloat16 [3072, 768], P('dp'), may hold values from -0.109375 to 0.109375
- down_bias: float32 [768], replicated, may hold values from -3 to 3
Outputs:
- block_output: float32 [4, 1024, 768], P('dp', 'ctx')
- input_grad: float32 [4, 1024, 768], P('dp', 'ctx')
- first_gain_grad: float32 [768], replicated
- first_shift_grad: float32 [768], replicated
- mix_weight_grad: float32 [768, 2304], P('dp')
- query_bias_grad: float32 [768], replicated
- value_bias_grad: float32 [768], replicated
- attn_weight_grad: float32 [768, 768], P('dp')
- attn_bias_grad: float32 [768], replicated
- second_gain_grad: float32 [768], replicated
- second_shift_grad: float32 [768], replicated
- up_weight_grad: float32 [768, 3072], P('dp')
- up_bias_grad: float32 [3072], replicated
- down_weight_grad: float32 [3072, 768], P('dp')
- down_bias_grad: float32 [768], replicated
The draws below stay inside these ranges and needn't reach their ends.
All inputs are finite; a program needn't handle non-finite values.
Results may differ from the reference program's by a relative error of at most 0.023.
Values may be sent and summed in bfloat16 or wider, within the bound.
A program may use at most 128 MiB of HBM per device.

```python
import math
import jax
import jax.numpy as jnp
from jax import lax

D = 768
H = 12
HD = 64
FF = 3072
LEN = 1024
SEQS = 4


def block_levels(rng, shape, cuts, low, largest):
    def one(axis_at, shards_of):
        draws = jax.random.uniform(jax.random.fold_in(jax.random.fold_in(rng, 6), axis_at), (shards_of,), jnp.float32, low / len(cuts), largest / len(cuts))
        return jnp.repeat(jnp.exp(draws), shape[axis_at] // shards_of).reshape((-1,) + (1,) * (len(shape) - axis_at - 1))

    level = one(*cuts[0])
    for cut in cuts[1:]:
        level = level * one(*cut)
    return level


def centred(rng, dims, scale, limit, split=(), held_as=jnp.bfloat16):
    level = block_levels(rng, dims, split, -0.22, 0.18) if split else 1.0
    entries = jax.random.normal(rng, dims, jnp.float32) * scale * level
    return jnp.minimum(jnp.maximum(entries, -limit), limit).astype(held_as)


def setup_inputs(seed: int = 0) -> dict:
    streams_of = jax.random.split(jax.random.key(seed), 16)
    block_input = centred(streams_of[0], (SEQS, LEN, D), 1.0, 6.0, ((0, 4), (1, 8)), jnp.float32)
    out_cotangent = centred(streams_of[1], (SEQS, LEN, D), 1.0, 6.0, ((0, 4), (1, 8)), jnp.float32)
    first_gain = jnp.clip(1.0 + 0.15 * jax.random.normal(streams_of[2], (D,), jnp.float32), 0.25, 1.75)
    first_shift = centred(streams_of[3], (D,), 0.5, 3.0, (), jnp.float32)
    mix_weight = centred(streams_of[4], (D, 3 * D), D ** -0.5, 0.21875, ((0, 4),))
    query_bias = centred(streams_of[5], (D,), 0.5, 3.0, (), jnp.float32)
    value_bias = centred(streams_of[6], (D,), 0.5, 3.0, (), jnp.float32)
    attn_weight = centred(streams_of[7], (D, D), HD ** -0.5, 0.75, ((0, 4),))
    attn_bias = centred(streams_of[8], (D,), 0.5, 3.0, (), jnp.float32)
    second_gain = jnp.clip(1.0 + 0.15 * jax.random.normal(streams_of[9], (D,), jnp.float32), 0.25, 1.75)
    second_shift = centred(streams_of[10], (D,), 0.5, 3.0, (), jnp.float32)
    up_weight = centred(streams_of[11], (D, FF), D ** -0.5, 0.21875, ((0, 4),))
    up_bias = centred(streams_of[12], (FF,), 0.5, 3.0, (), jnp.float32)
    down_weight = centred(streams_of[13], (FF, D), FF ** -0.5, 0.109375, ((0, 4),))
    down_bias = centred(streams_of[14], (D,), 0.5, 3.0, (), jnp.float32)
    return dict(block_input=block_input, out_cotangent=out_cotangent, first_gain=first_gain, first_shift=first_shift, mix_weight=mix_weight, query_bias=query_bias, value_bias=value_bias, attn_weight=attn_weight, attn_bias=attn_bias, second_gain=second_gain, second_shift=second_shift, up_weight=up_weight, up_bias=up_bias, down_weight=down_weight, down_bias=down_bias)


EPS = 1e-05
GELU_C = math.sqrt(2.0 / math.pi)

def layer_norm(x, gain, shift):
    centered = x - lax.optimization_barrier(jnp.mean(x, axis=-1, keepdims=True))
    rstd = lax.rsqrt(lax.optimization_barrier(jnp.mean(centered * centered, axis=-1, keepdims=True)) + EPS)
    x_hat = centered * rstd
    return (x_hat, rstd, x_hat * gain + shift)

def norm_back(grad, x_hat, rstd, gain):
    g = grad * gain
    return rstd * (g - lax.optimization_barrier(jnp.mean(g, axis=-1, keepdims=True)) - x_hat * lax.optimization_barrier(jnp.mean(g * x_hat, axis=-1, keepdims=True)))

def gelu_pair(u):
    inner = GELU_C * (u + 0.044715 * u * u * u)
    t = jnp.tanh(inner)
    value = 0.5 * u * (1.0 + t)
    slope = 0.5 * (1.0 + t) + 0.5 * u * (1.0 - t * t) * GELU_C * (1.0 + 3.0 * 0.044715 * u * u)
    return (value, slope)

def matmul(a, b):
    return jnp.dot(a, b, preferred_element_type=jnp.float32)

def matmul_tn(a, b):
    return jnp.dot(a.T, b, preferred_element_type=jnp.float32)

def matmul_nt(a, b):
    return jnp.dot(a, b.T, preferred_element_type=jnp.float32)

def attention_forward(queries, keys, values):
    length = queries.shape[0]
    qblock = math.gcd(length, 512)
    nblocks = length // qblock
    scale = HD ** (-0.5)
    keys_f = keys.astype(jnp.float32)
    values_f = values.astype(jnp.float32)
    key_pos = jnp.arange(length).astype(jnp.int32)

    def one_block(index):
        start = (index * qblock).astype(jnp.int32)
        q_blk = lax.dynamic_slice_in_dim(queries, start, qblock, 0).astype(jnp.float32)
        scores = jnp.einsum('qhd,khd->hqk', q_blk, keys_f) * scale
        q_pos = start + jnp.arange(qblock).astype(jnp.int32)
        allowed = (key_pos[None, :] <= q_pos[:, None])[None]
        scores = jnp.where(allowed, scores, -1e+30)
        row_max = lax.optimization_barrier(jnp.max(scores, axis=-1))
        expo = jnp.where(allowed, jnp.exp(scores - row_max[..., None]), 0.0)
        total = lax.optimization_barrier(jnp.sum(expo, axis=-1))
        out = jnp.einsum('hqk,khd->qhd', expo, values_f, precision=lax.Precision.HIGHEST) / total.T[..., None]
        return (out, row_max + jnp.log(total))
    outs, lses = lax.map(one_block, jnp.arange(nblocks).astype(jnp.int32))
    attended = outs.reshape(length, H * HD).astype(jnp.bfloat16)
    lse = jnp.transpose(lses, (1, 0, 2)).reshape(H, length)
    return (attended, lse)

def attention_backward(queries, keys, values, attended, lse, attended_grad):
    length = queries.shape[0]
    qblock = math.gcd(length, 512)
    nblocks = length // qblock
    scale = HD ** (-0.5)
    keys_f = keys.astype(jnp.float32)
    values_f = values.astype(jnp.float32)
    grad_f = attended_grad.astype(jnp.float32).reshape(length, H, HD)
    delta = lax.optimization_barrier(jnp.sum(grad_f * attended.astype(jnp.float32).reshape(length, H, HD), axis=-1))
    key_pos = jnp.arange(length).astype(jnp.int32)

    def one_block(carry, index):
        key_acc, value_acc = carry
        start = (index * qblock).astype(jnp.int32)
        q_blk = lax.dynamic_slice_in_dim(queries, start, qblock, 0).astype(jnp.float32)
        g_blk = lax.dynamic_slice_in_dim(grad_f, start, qblock, 0)
        d_blk = lax.dynamic_slice_in_dim(delta, start, qblock, 0)
        l_blk = lax.dynamic_slice_in_dim(lse, start, qblock, 1)
        scores = jnp.einsum('qhd,khd->hqk', q_blk, keys_f) * scale
        q_pos = start + jnp.arange(qblock).astype(jnp.int32)
        allowed = (key_pos[None, :] <= q_pos[:, None])[None]
        probs = jnp.where(allowed, jnp.exp(scores - l_blk[..., None]), 0.0)
        dprob = jnp.einsum('qhd,khd->hqk', g_blk, values_f)
        dscore = probs * (dprob - d_blk.T[..., None])
        probs_b = probs.astype(jnp.bfloat16).astype(jnp.float32)
        dscore_b = dscore.astype(jnp.bfloat16).astype(jnp.float32)
        value_acc = value_acc + jnp.einsum('hqk,qhd->khd', probs_b, g_blk)
        key_acc = key_acc + jnp.einsum('hqk,qhd->khd', dscore_b, q_blk) * scale
        q_grad = jnp.einsum('hqk,khd->qhd', dscore_b, keys_f) * scale
        return ((key_acc, value_acc), q_grad)
    zeros = jnp.zeros((length, H, HD), jnp.float32)
    (key_grad, value_grad), q_grads = lax.scan(one_block, (zeros, zeros), jnp.arange(nblocks).astype(jnp.int32))
    query_grad = q_grads.reshape(length, H * HD)
    return (query_grad, key_grad.reshape(length, H * HD), value_grad.reshape(length, H * HD))

def one_sequence(x, cot, params):
    first_gain, first_shift, mix_weight, query_bias, value_bias, attn_weight, attn_bias, second_gain, second_shift, up_weight, up_bias, down_weight, down_bias = params
    width = x.shape[1]
    length = x.shape[0]
    first_hat, first_rstd, first_out = layer_norm(x, first_gain, first_shift)
    first_in = first_out.astype(jnp.bfloat16)
    mixed = matmul(first_in, mix_weight)
    queries = (mixed[:, :width] + query_bias).astype(jnp.bfloat16)
    keys = mixed[:, width:2 * width].astype(jnp.bfloat16)
    values = (mixed[:, 2 * width:] + value_bias).astype(jnp.bfloat16)
    q3 = queries.reshape(length, H, HD)
    k3 = keys.reshape(length, H, HD)
    v3 = values.reshape(length, H, HD)
    attended, lse = attention_forward(q3, k3, v3)
    after_attn = x + matmul(attended, attn_weight) + attn_bias
    second_hat, second_rstd, second_out = layer_norm(after_attn, second_gain, second_shift)
    second_in = second_out.astype(jnp.bfloat16)
    pre_act = matmul(second_in, up_weight) + up_bias
    act_value, act_slope = gelu_pair(pre_act)
    activ = act_value.astype(jnp.bfloat16)
    block_output = after_attn + matmul(activ, down_weight) + down_bias
    cot_b = cot.astype(jnp.bfloat16)
    down_weight_grad = matmul_tn(activ, cot_b)
    down_bias_grad = lax.optimization_barrier(jnp.sum(cot, axis=0))
    pre_grad = matmul_nt(cot_b, down_weight) * act_slope
    pre_grad_b = pre_grad.astype(jnp.bfloat16)
    up_weight_grad = matmul_tn(second_in, pre_grad_b)
    up_bias_grad = lax.optimization_barrier(jnp.sum(pre_grad, axis=0))
    second_grad = matmul_nt(pre_grad_b, up_weight)
    second_gain_grad = lax.optimization_barrier(jnp.sum(second_grad * second_hat, axis=0))
    second_shift_grad = lax.optimization_barrier(jnp.sum(second_grad, axis=0))
    resid_grad = cot + norm_back(second_grad, second_hat, second_rstd, second_gain)
    resid_b = resid_grad.astype(jnp.bfloat16)
    attn_weight_grad = matmul_tn(attended, resid_b)
    attn_bias_grad = lax.optimization_barrier(jnp.sum(resid_grad, axis=0))
    attended_grad = matmul_nt(resid_b, attn_weight).astype(jnp.bfloat16)
    query_grad, key_grad, value_grad = attention_backward(q3, k3, v3, attended, lse, attended_grad)
    query_bias_grad = lax.optimization_barrier(jnp.sum(query_grad, axis=0))
    value_bias_grad = lax.optimization_barrier(jnp.sum(value_grad, axis=0))
    mixed_grad = jnp.concatenate([query_grad, key_grad, value_grad], axis=1).astype(jnp.bfloat16)
    mix_weight_grad = matmul_tn(first_in, mixed_grad)
    first_grad = matmul_nt(mixed_grad, mix_weight)
    first_gain_grad = lax.optimization_barrier(jnp.sum(first_grad * first_hat, axis=0))
    first_shift_grad = lax.optimization_barrier(jnp.sum(first_grad, axis=0))
    input_grad = resid_grad + norm_back(first_grad, first_hat, first_rstd, first_gain)
    grads = (first_gain_grad, first_shift_grad, mix_weight_grad, query_bias_grad, value_bias_grad, attn_weight_grad, attn_bias_grad, second_gain_grad, second_shift_grad, up_weight_grad, up_bias_grad, down_weight_grad, down_bias_grad)
    return (block_output, input_grad, grads)

def reference(block_input, out_cotangent, first_gain, first_shift, mix_weight, query_bias, value_bias, attn_weight, attn_bias, second_gain, second_shift, up_weight, up_bias, down_weight, down_bias):
    params = (first_gain, first_shift, mix_weight, query_bias, value_bias, attn_weight, attn_bias, second_gain, second_shift, up_weight, up_bias, down_weight, down_bias)
    zero_grads = tuple((jnp.zeros(p.shape, jnp.float32) for p in params))

    def step(carry, item):
        x, cot = item
        out, in_grad, grads = one_sequence(x, cot, params)
        carry = tuple((c + g for c, g in zip(carry, grads)))
        return (carry, (out, in_grad))
    totals, (outputs, input_grads) = lax.scan(step, zero_grads, (block_input, out_cotangent))
    return (outputs, input_grads, totals[0], totals[1], totals[2], totals[3], totals[4], totals[5], totals[6], totals[7], totals[8], totals[9], totals[10], totals[11], totals[12])
```

```python
import functools
import math

import jax
import jax.numpy as jnp
from jax import lax
from jax.experimental import pallas as pl
from jax.experimental.pallas import tpu as pltpu
from jax.sharding import PartitionSpec as P

H = 12
HD = 64


EPS = 1e-05
GELU_C = math.sqrt(2.0 / math.pi)


def from_behind(value, axis, steps):
    count = lax.axis_size(axis)
    pairs = [(source, (source + steps) % count) for source in range(count)]
    return lax.ppermute(value, axis, pairs)


def layer_norm(x, gain, shift):
    centered = x - jnp.mean(x, axis=-1, keepdims=True)
    rstd = lax.rsqrt(jnp.mean(centered * centered, axis=-1, keepdims=True) + EPS)
    x_hat = centered * rstd
    return (x_hat, rstd, x_hat * gain + shift)


def norm_back(grad, x_hat, rstd, gain):
    g = grad * gain
    return rstd * (
        g
        - jnp.mean(g, axis=-1, keepdims=True)
        - x_hat * jnp.mean(g * x_hat, axis=-1, keepdims=True)
    )


def gelu_pair(u):
    inner = GELU_C * (u + 0.044715 * u * u * u)
    t = jnp.tanh(inner)
    value = 0.5 * u * (1.0 + t)
    slope = 0.5 * (1.0 + t) + 0.5 * u * (1.0 - t * t) * GELU_C * (1.0 + 3.0 * 0.044715 * u * u)
    return (value, slope)


def matmul(a, b):
    return jnp.dot(a, b, preferred_element_type=jnp.float32)


def matmul_tn(a, b):
    return lax.dot_general(a, b, (((0,), (0,)), ((), ())), preferred_element_type=jnp.float32)


def matmul_nt(a, b):
    return lax.dot_general(a, b, (((1,), (1,)), ((), ())), preferred_element_type=jnp.float32)


def body(
    block_input,
    out_cotangent,
    first_gain,
    first_shift,
    mix_weight,
    query_bias,
    value_bias,
    attn_weight,
    attn_bias,
    second_gain,
    second_shift,
    up_weight,
    up_bias,
    down_weight,
    down_bias,
):
    rows = block_input.shape[1]
    width = block_input.shape[2]
    scale = HD ** (-0.5)
    x_rows = block_input.reshape(rows, width)
    cot = out_cotangent.reshape(rows, width)
    mix_full, attn_full, up_full, down_full = (
        lax.all_gather(mix_weight, "dp", axis=0, tiled=True),
        lax.all_gather(attn_weight, "dp", axis=0, tiled=True),
        lax.all_gather(up_weight, "dp", axis=0, tiled=True),
        lax.all_gather(down_weight, "dp", axis=0, tiled=True),
    )
    first_hat, first_rstd, first_out = layer_norm(x_rows, first_gain, first_shift)
    first_in = first_out.astype(jnp.bfloat16)
    mixed = matmul(first_in, mix_full)
    queries = (mixed[:, :width] + query_bias).astype(jnp.bfloat16)
    keys = mixed[:, width : 2 * width].astype(jnp.bfloat16)
    values = (mixed[:, 2 * width :] + value_bias).astype(jnp.bfloat16)
    q3 = queries.reshape(rows, H, HD)
    me = lax.axis_index("ctx")
    cycle_size = lax.axis_size("ctx")
    q_pos = me * rows + jnp.arange(rows)
    q_last = me * rows + rows - 1
    start_state = (
        jnp.full((H, rows), -1e30, jnp.float32),
        jnp.zeros((H, rows), jnp.float32),
        jnp.zeros((H, rows, HD), jnp.float32),
    )
    carry = start_state
    key_piece = lax.all_gather(keys, "ctx", axis=0, tiled=True)
    value_piece = lax.all_gather(values, "ctx", axis=0, tiled=True)
    count = key_piece.shape[0]
    kblock = math.gcd(count, 512)
    nblocks = count // kblock
    key_blocks = key_piece.reshape(nblocks, kblock, H, HD)
    value_blocks = value_piece.reshape(nblocks, kblock, H, HD)
    offsets = jnp.arange(nblocks) * kblock

    def one_block(state, item):
        key_blk, value_blk, offset = item

        def compute(state_in):
            run_max, run_total, run_acc = state_in
            key_pos = offset + jnp.arange(kblock)
            allowed = (key_pos[None, :] <= q_pos[:, None])[None]
            scores = (
                jnp.einsum("qhd,khd->hqk", q3, key_blk, preferred_element_type=jnp.float32) * scale
            )
            scores = jnp.where(allowed, scores, -1e30)
            new_max = jnp.maximum(run_max, jnp.max(scores, axis=-1))
            expo = jnp.where(allowed, jnp.exp(scores - new_max[..., None]), 0.0)
            factor = jnp.exp(run_max - new_max)
            new_total = run_total * factor + jnp.sum(expo, axis=-1)
            new_acc = run_acc * factor[..., None] + jnp.einsum(
                "hqk,khd->hqd", expo, value_blk.astype(jnp.float32), precision=lax.Precision.HIGHEST
            )
            return (new_max, new_total, new_acc)

        def keep_state(state_in):
            return state_in

        return (lax.cond(offset <= q_last, compute, keep_state, state), None)

    carry, unused = lax.scan(one_block, carry, (key_blocks, value_blocks, offsets))
    run_max, run_total, run_acc = carry
    attended = (
        (run_acc / run_total[..., None])
        .transpose(1, 0, 2)
        .reshape(rows, width)
        .astype(jnp.bfloat16)
    )
    lse = run_max + jnp.log(run_total)
    after_attn = x_rows + matmul(attended, attn_full) + attn_bias
    second_hat, second_rstd, second_out = layer_norm(after_attn, second_gain, second_shift)
    second_in = second_out.astype(jnp.bfloat16)
    pre_act = matmul(second_in, up_full) + up_bias
    act_value, act_slope = gelu_pair(pre_act)
    activ = act_value.astype(jnp.bfloat16)
    block_output = after_attn + matmul(activ, down_full) + down_bias
    mix_back, attn_back, up_back, down_back = (
        lax.all_gather(mix_weight, "dp", axis=0, tiled=True),
        lax.all_gather(attn_weight, "dp", axis=0, tiled=True),
        lax.all_gather(up_weight, "dp", axis=0, tiled=True),
        lax.all_gather(down_weight, "dp", axis=0, tiled=True),
    )
    cot_b = cot.astype(jnp.bfloat16)
    down_weight_grad = matmul_tn(activ, cot_b)
    down_bias_grad = jnp.sum(cot, axis=0)
    pre_grad = matmul_nt(cot_b, down_back) * act_slope
    pre_grad_b = pre_grad.astype(jnp.bfloat16)
    up_weight_grad = matmul_tn(second_in, pre_grad_b)
    up_bias_grad = jnp.sum(pre_grad, axis=0)
    second_grad = matmul_nt(pre_grad_b, up_back)
    second_gain_grad = jnp.sum(second_grad * second_hat, axis=0)
    second_shift_grad = jnp.sum(second_grad, axis=0)
    resid_grad = cot + norm_back(second_grad, second_hat, second_rstd, second_gain)
    resid_b = resid_grad.astype(jnp.bfloat16)
    attn_weight_grad = matmul_tn(attended, resid_b)
    attn_bias_grad = jnp.sum(resid_grad, axis=0)
    attended_grad = matmul_nt(resid_b, attn_back).astype(jnp.bfloat16)
    grad3 = attended_grad.reshape(rows, H, HD)
    delta = jnp.sum(
        grad3.astype(jnp.float32) * attended.astype(jnp.float32).reshape(rows, H, HD), axis=-1
    ).T

    def block_grads(key_blk, value_blk, key_start):
        count = key_blk.shape[0]
        key3 = key_blk.reshape(count, H, HD)
        value3 = value_blk.reshape(count, H, HD)
        key_pos = key_start + jnp.arange(count)
        allowed = (key_pos[None, :] <= q_pos[:, None])[None]
        scores = jnp.einsum("qhd,khd->hqk", q3, key3, preferred_element_type=jnp.float32) * scale
        probs = jnp.where(allowed, jnp.exp(scores - lse[..., None]), 0.0)
        dprob = jnp.einsum("qhd,khd->hqk", grad3, value3, preferred_element_type=jnp.float32)
        dscore = probs * (dprob - delta[..., None])
        probs_b = probs.astype(jnp.bfloat16)
        dscore_b = dscore.astype(jnp.bfloat16)
        value_add = jnp.einsum("hqk,qhd->khd", probs_b, grad3, preferred_element_type=jnp.float32)
        key_add = (
            jnp.einsum("hqk,qhd->khd", dscore_b, q3, preferred_element_type=jnp.float32) * scale
        )
        query_add = (
            jnp.einsum("hqk,khd->qhd", dscore_b, key3, preferred_element_type=jnp.float32) * scale
        )
        return (
            query_add.reshape(rows, width),
            key_add.reshape(count, width),
            value_add.reshape(count, width),
        )

    def skip_grads(key_blk, value_blk, key_start):
        count = key_blk.shape[0]
        empty = jnp.zeros((count, width), jnp.float32)
        return (jnp.zeros((rows, width), jnp.float32), empty, empty)

    zeros = jnp.zeros((rows, width), jnp.float32)

    def pass_grads(key_acc, value_acc):
        return (
            from_behind(key_acc.astype(jnp.bfloat16), "ctx", -1).astype(key_acc.dtype),
            from_behind(value_acc.astype(jnp.bfloat16), "ctx", -1).astype(value_acc.dtype),
        )

    def cycle_turn(step, state):
        key_blk, value_blk, key_acc, value_acc, query_acc = state
        owner = (me + step) % cycle_size
        query_add, key_add, value_add = lax.cond(
            owner <= me, block_grads, skip_grads, key_blk, value_blk, owner * rows
        )
        key_blk, value_blk = from_behind((key_blk, value_blk), "ctx", -1)
        key_acc, value_acc = pass_grads(key_acc + key_add, value_acc + value_add)
        return (key_blk, value_blk, key_acc, value_acc, query_acc + query_add)

    key_blk, value_blk, key_acc, value_acc, query_acc = lax.fori_loop(
        0, cycle_size - 1, cycle_turn, (keys, values, zeros, zeros, zeros)
    )
    last_owner = (me + cycle_size - 1) % cycle_size
    query_add, key_add, value_add = lax.cond(
        last_owner <= me, block_grads, skip_grads, key_blk, value_blk, last_owner * rows
    )
    key_grad, value_grad = pass_grads(key_acc + key_add, value_acc + value_add)
    query_grad = query_acc + query_add
    query_bias_grad = jnp.sum(query_grad, axis=0)
    value_bias_grad = jnp.sum(value_grad, axis=0)
    mixed_grad = jnp.concatenate([query_grad, key_grad, value_grad], axis=1).astype(jnp.bfloat16)
    mix_weight_grad = matmul_tn(first_in, mixed_grad)
    first_grad = matmul_nt(mixed_grad, mix_back)
    first_gain_grad = jnp.sum(first_grad * first_hat, axis=0)
    first_shift_grad = jnp.sum(first_grad, axis=0)
    input_grad = resid_grad + norm_back(first_grad, first_hat, first_rstd, first_gain)
    local_mats = (mix_weight_grad, attn_weight_grad, up_weight_grad, down_weight_grad)
    shard_sums = (
        lax.psum_scatter(
            local_mats[0].astype(jnp.bfloat16), "dp", scatter_dimension=0, tiled=True
        ).astype(jnp.float32),
        lax.psum_scatter(
            local_mats[1].astype(jnp.bfloat16), "dp", scatter_dimension=0, tiled=True
        ).astype(jnp.float32),
        lax.psum_scatter(
            local_mats[2].astype(jnp.bfloat16), "dp", scatter_dimension=0, tiled=True
        ).astype(jnp.float32),
        lax.psum_scatter(
            local_mats[3].astype(jnp.bfloat16), "dp", scatter_dimension=0, tiled=True
        ).astype(jnp.float32),
    )
    mats = (
        lax.psum(shard_sums[0].astype(jnp.bfloat16), "ctx").astype(jnp.float32),
        lax.psum(shard_sums[1].astype(jnp.bfloat16), "ctx").astype(jnp.float32),
        lax.psum(shard_sums[2].astype(jnp.bfloat16), "ctx").astype(jnp.float32),
        lax.psum(shard_sums[3].astype(jnp.bfloat16), "ctx").astype(jnp.float32),
    )
    smalls = lax.psum(
        (
            first_gain_grad,
            first_shift_grad,
            query_bias_grad,
            value_bias_grad,
            attn_bias_grad,
            second_gain_grad,
            second_shift_grad,
            up_bias_grad,
            down_bias_grad,
        ),
        ("dp", "ctx"),
    )
    return (
        block_output.reshape(1, rows, width),
        input_grad.reshape(1, rows, width),
        smalls[0],
        smalls[1],
        mats[0],
        smalls[2],
        smalls[3],
        mats[1],
        smalls[4],
        smalls[5],
        smalls[6],
        mats[2],
        smalls[7],
        mats[3],
        smalls[8],
    )


def flip(index, mask):
    bit = 1
    while bit <= mask:
        if mask & bit:
            index = index + bit - 2 * bit * ((index // bit) % 2)
        bit *= 2
    return index


def group_size(group, sizes):
    return {"dp": sizes[0], "z": sizes[1] // 2, "core": 2}[group]


def exchange_kernel(plan, sizes, *refs):
    count = len(plan)
    ins, outs = refs[:count], refs[count : 2 * count]
    send_sem, recv_sem, local_sem = refs[2 * count :]
    dp, ctx = lax.axis_index("dp"), lax.axis_index("ctx")
    slots = {"dp": dp, "z": ctx // 2, "core": ctx % 2}

    def peer(group, step):
        if group == "dp":
            return (flip(dp, step), ctx)
        return (dp, flip(ctx, 2 * step if group == "z" else step))

    barrier = pltpu.get_barrier_semaphore()
    greeted = 0
    for group in sorted({group for group, mode in plan}):
        for step in range(1, group_size(group, sizes)):
            pl.semaphore_signal(
                barrier, inc=1, device_id=peer(group, step), device_id_type=pl.DeviceIdType.MESH
            )
            greeted += 1
    pl.semaphore_wait(barrier, greeted)
    copies = []
    for item, (group, mode) in enumerate(plan):
        me = slots[group]
        for step in range(group_size(group, sizes) - 1, 0, -1):
            source = ins[item].at[flip(me, step)] if mode == "a2a" else ins[item]
            copy = pltpu.make_async_remote_copy(
                src_ref=source,
                dst_ref=outs[item].at[me],
                send_sem=send_sem.at[item, step],
                recv_sem=recv_sem.at[item, step],
                device_id=peer(group, step),
                device_id_type=pl.DeviceIdType.MESH,
            )
            copy.start()
            copies.append(copy)
    for item, (group, mode) in enumerate(plan):
        me = slots[group]
        source = ins[item].at[me] if mode == "a2a" else ins[item]
        copy = pltpu.make_async_copy(source, outs[item].at[me], local_sem.at[item])
        copy.start()
        copies.append(copy)
    for copy in copies:
        copy.wait()


def exchange(number, *items):
    sizes = (lax.axis_size("dp"), lax.axis_size("ctx"))
    plan = tuple((group, mode) for group, mode, value in items)
    values = [value for group, mode, value in items]
    shapes = [
        jax.ShapeDtypeStruct(
            value.shape if mode == "a2a" else (group_size(group, sizes),) + value.shape, value.dtype
        )
        for group, mode, value in items
    ]
    most = max(group_size(group, sizes) for group, mode in plan)
    return pl.pallas_call(
        functools.partial(exchange_kernel, plan, sizes),
        out_shape=shapes,
        in_specs=[pl.BlockSpec(memory_space=pltpu.VMEM)] * len(values),
        out_specs=[pl.BlockSpec(memory_space=pl.ANY)] * len(values),
        scratch_shapes=[
            pltpu.SemaphoreType.DMA((len(values), most)),
            pltpu.SemaphoreType.DMA((len(values), most)),
            pltpu.SemaphoreType.DMA((len(values),)),
        ],
        compiler_params=pltpu.CompilerParams(collective_id=number, has_side_effects=True),
        name="exchange_%d" % number,
    )(*values)


def attend_kernel(scale, q_ref, k_ref, v_ref, qpos_ref, kpos_ref, out_ref, lse_ref):
    scores = matmul_nt(q_ref[0], k_ref[0]) * scale
    allowed = kpos_ref[...] <= qpos_ref[...]
    scores = jnp.where(allowed, scores, -1e30)
    top = jnp.max(scores, axis=-1, keepdims=True)
    weights = jnp.exp(scores - top)
    total = jnp.sum(weights, axis=-1, keepdims=True)
    mixed = matmul(weights.astype(jnp.bfloat16), v_ref[0])
    out_ref[0] = (mixed / total).astype(jnp.bfloat16)
    lse_ref[0] = top + jnp.log(total)


def attend_back_kernel(
    scale, q_ref, k_ref, v_ref, qpos_ref, kpos_ref, out_ref, lse_ref, grad_ref, dq_ref, dk_ref, dv_ref
):
    q, k, v, grad = q_ref[0], k_ref[0], v_ref[0], grad_ref[0]
    delta = jnp.sum(
        grad.astype(jnp.float32) * out_ref[0].astype(jnp.float32), axis=-1, keepdims=True
    )
    scores = matmul_nt(q, k) * scale
    allowed = kpos_ref[...] <= qpos_ref[...]
    probs = jnp.where(allowed, jnp.exp(scores - lse_ref[0]), 0.0)
    dprob = matmul_nt(grad, v)
    dscore = (probs * (dprob - delta)).astype(jnp.bfloat16)
    dv_ref[0] = matmul_tn(probs.astype(jnp.bfloat16), grad)
    dk_ref[0] = matmul_tn(dscore, q) * scale
    dq_ref[0] = matmul(dscore, k) * scale


def per_head(kernel, name, heads, inputs, shared, outs):
    def whole(shape):
        return pl.BlockSpec(shape, lambda h: (0,) * len(shape))

    def one(shape):
        return pl.BlockSpec((1,) + shape[1:], lambda h: (h, 0, 0))

    order = [(value, one(value.shape)) for value in inputs[:3]]
    order += [(value, whole(value.shape)) for value in shared]
    order += [(value, one(value.shape)) for value in inputs[3:]]
    return pl.pallas_call(
        kernel,
        grid=(heads,),
        out_shape=[jax.ShapeDtypeStruct(shape, dtype) for shape, dtype in outs],
        in_specs=[spec for value, spec in order],
        out_specs=[one(shape) for shape, dtype in outs],
        name=name,
    )(*[value for value, spec in order])


def tensor_body(
    block_input,
    out_cotangent,
    first_gain,
    first_shift,
    mix_weight,
    query_bias,
    value_bias,
    attn_weight,
    attn_bias,
    second_gain,
    second_shift,
    up_weight,
    up_bias,
    down_weight,
    down_bias,
):
    b16, f32 = jnp.bfloat16, jnp.float32
    n, nz = lax.axis_size("dp"), lax.axis_size("ctx") // 2
    rows, width = block_input.shape[1:]
    total_rows = n * rows
    shard = width // n
    heads = H // n
    hidden = up_weight.shape[1] // n
    scale = HD ** (-0.5)
    dp, core = lax.axis_index("dp"), lax.axis_index("ctx") % 2
    x_rows = block_input.reshape(rows, width)
    cot = out_cotangent.reshape(rows, width)
    cot_b = cot.astype(b16)

    def total(value):
        return jnp.sum(value.astype(f32), axis=0)

    first_hat, first_rstd, first_out = layer_norm(x_rows, first_gain, first_shift)
    mix_parts = mix_weight.reshape(shard, 3, n, shard).transpose(2, 0, 1, 3).reshape(n, shard, 3 * shard)
    up_parts = up_weight.reshape(shard, n, hidden).transpose(1, 0, 2)
    mix_cols, first_all = exchange(
        0, ("dp", "a2a", mix_parts), ("dp", "ag", first_out.astype(b16))
    )
    mix_cols = mix_cols.reshape(width, 3 * shard)
    first_all = first_all.reshape(total_rows, width)
    own = lambda vector, size: lax.dynamic_slice(vector, (dp * size,), (size,))
    mix_bias = jnp.concatenate(
        [own(query_bias, shard), jnp.zeros((shard,), f32), own(value_bias, shard)]
    )
    mixed = (matmul(first_all, mix_cols) + mix_bias).astype(b16)
    mixed_seq, up_cols, cot_all = exchange(
        1,
        ("z", "a2a", mixed.reshape(n, rows, 3 * shard)),
        ("dp", "a2a", up_parts),
        ("dp", "ag", cot_b),
    )
    up_cols = up_cols.reshape(width, hidden)
    cot_all = cot_all.reshape(total_rows, width)
    (kv_seq,) = exchange(2, ("core", "ag", mixed_seq[:, :, shard:]))

    def split_heads(value):
        return value.reshape(-1, heads, HD).transpose(1, 0, 2)

    def join_heads(value):
        return value.transpose(1, 0, 2).reshape(-1, shard)

    q_rows, k_rows = nz * rows, 2 * nz * rows
    kv_flat = kv_seq.reshape(k_rows, 2 * shard)
    q3 = split_heads(mixed_seq[:, :, :shard])
    k3, v3 = split_heads(kv_flat[:, :shard]), split_heads(kv_flat[:, shard:])
    q_idx, k_idx = jnp.arange(q_rows), jnp.arange(k_rows)
    q_pos = ((q_idx // rows) * 2 + core) * rows + q_idx % rows
    k_pos = (((k_idx % q_rows) // rows) * 2 + k_idx // q_rows) * rows + k_idx % rows
    shared = (q_pos.astype(jnp.int32)[:, None], k_pos.astype(jnp.int32)[None, :])
    out3, lse = per_head(
        functools.partial(attend_kernel, scale),
        "attend",
        heads,
        (q3, k3, v3),
        shared,
        (((heads, q_rows, HD), b16), ((heads, q_rows, 1), f32)),
    )
    (attended,) = exchange(3, ("z", "a2a", join_heads(out3).reshape(nz, rows, shard)))
    attended = attended.reshape(total_rows, shard)
    (attn_parts,) = exchange(
        4, ("dp", "a2a", matmul(attended, attn_weight).astype(b16).reshape(n, rows, width))
    )
    after_attn = x_rows + total(attn_parts) + attn_bias
    second_hat, second_rstd, second_out = layer_norm(after_attn, second_gain, second_shift)
    (second_all,) = exchange(5, ("dp", "ag", second_out.astype(b16)))
    second_all = second_all.reshape(total_rows, width)
    pre_act = matmul(second_all, up_cols) + own(up_bias, hidden)
    act_value, act_slope = gelu_pair(pre_act)
    activ = act_value.astype(b16)
    out_part = matmul(activ, down_weight).astype(b16)
    pre_grad = matmul_nt(cot_all, down_weight) * act_slope
    pre_grad_b = pre_grad.astype(b16)
    second_part = matmul_nt(pre_grad_b, up_cols).astype(b16)
    down_grad = matmul_tn(activ, cot_all).astype(b16)
    up_grad = matmul_tn(second_all, pre_grad_b).astype(b16)
    up_bias_grad = jnp.sum(pre_grad, axis=0)

    def halves(value):
        return value.reshape(value.shape[0], 2, -1).transpose(1, 0, 2)

    out_parts, second_parts, down_pair, up_pair = exchange(
        6,
        ("dp", "a2a", out_part.reshape(n, rows, width)),
        ("dp", "a2a", second_part.reshape(n, rows, width)),
        ("core", "a2a", halves(down_grad)),
        ("core", "a2a", halves(up_grad)),
    )
    block_output = after_attn + total(out_parts) + down_bias
    second_grad = total(second_parts)
    resid_grad = cot + norm_back(second_grad, second_hat, second_rstd, second_gain)
    down_sum = total(down_pair).astype(b16).reshape(nz, hidden // nz, width // 2)

    def by_rows(value):
        columns = value.shape[-1]
        return value.reshape(n, nz, shard // nz, columns).transpose(1, 0, 2, 3)

    up_sum = by_rows(total(up_pair).astype(b16))
    resid_all, down_z, up_z = exchange(
        7,
        ("dp", "ag", resid_grad.astype(b16)),
        ("z", "a2a", down_sum),
        ("z", "a2a", up_sum),
    )
    resid_all = resid_all.reshape(total_rows, width)
    attended_grad = matmul_nt(resid_all, attn_weight).astype(b16)
    attn_grad = matmul_tn(attended, resid_all).astype(b16)
    down_piece = total(down_z).astype(b16)
    up_piece = total(up_z).astype(b16)
    grad_seq, up_dp, attn_pair = exchange(
        8,
        ("z", "a2a", attended_grad.reshape(n, rows, shard)),
        ("dp", "a2a", up_piece),
        ("core", "a2a", halves(attn_grad)),
    )
    dq3, dk3, dv3 = per_head(
        functools.partial(attend_back_kernel, scale),
        "attend_back",
        heads,
        (q3, k3, v3, out3, lse, split_heads(grad_seq)),
        shared,
        (((heads, q_rows, HD), f32), ((heads, k_rows, HD), f32), ((heads, k_rows, HD), f32)),
    )
    query_sum = jnp.sum(dq3, axis=1).reshape(shard)
    value_sum = jnp.sum(dv3, axis=1).reshape(shard)
    key_value = jnp.concatenate([join_heads(dk3), join_heads(dv3)], axis=1).astype(b16)
    (kv_pair,) = exchange(9, ("core", "a2a", key_value.reshape(2, nz, rows, 2 * shard)))
    mixed_back = jnp.concatenate(
        [join_heads(dq3).astype(b16).reshape(nz, rows, shard), total(kv_pair).astype(b16)], axis=-1
    )
    attn_sum = total(attn_pair).astype(b16).reshape(nz, shard // nz, width // 2)
    mixed_grad, attn_z = exchange(10, ("z", "a2a", mixed_back), ("z", "a2a", attn_sum))
    mixed_grad = mixed_grad.reshape(total_rows, 3 * shard)
    first_part = matmul_nt(mixed_grad, mix_cols).astype(b16)
    mix_grad = matmul_tn(first_all, mixed_grad).astype(b16)
    attn_piece = total(attn_z).astype(b16)
    first_parts, mix_pair, down_all, up_all, attn_all = exchange(
        11,
        ("dp", "a2a", first_part.reshape(n, rows, width)),
        ("core", "a2a", halves(mix_grad)),
        ("z", "ag", down_piece),
        ("z", "ag", up_dp),
        ("z", "ag", attn_piece),
    )
    first_grad = total(first_parts)
    input_grad = resid_grad + norm_back(first_grad, first_hat, first_rstd, first_gain)

    def spread(vector, full):
        return lax.dynamic_update_slice(
            jnp.zeros((full,), f32), vector, (dp * vector.shape[0],)
        )

    smalls = [
        jnp.sum(first_grad * first_hat, axis=0),
        jnp.sum(first_grad, axis=0),
        spread(query_sum, width),
        spread(value_sum, width),
        jnp.sum(resid_grad, axis=0),
        jnp.sum(second_grad * second_hat, axis=0),
        jnp.sum(second_grad, axis=0),
        spread(up_bias_grad, hidden * n),
        jnp.sum(cot, axis=0),
    ]
    lengths = [vector.shape[0] for vector in smalls]
    small = jnp.concatenate(smalls).reshape(-1, 128)
    mix_sum = by_rows(total(mix_pair).astype(b16))
    mix_z, small_pair, down_full, up_full, attn_full = exchange(
        12,
        ("z", "a2a", mix_sum),
        ("core", "ag", small),
        ("core", "ag", down_all),
        ("core", "ag", up_all),
        ("core", "ag", attn_all),
    )
    mix_dp, small_z = exchange(
        13, ("dp", "a2a", total(mix_z).astype(b16)), ("z", "ag", total(small_pair))
    )
    mix_all, small_dp = exchange(14, ("z", "ag", mix_dp), ("dp", "ag", total(small_z)))
    (mix_full,) = exchange(15, ("core", "ag", mix_all))
    small = total(small_dp).reshape(-1)
    vectors, start = [], 0
    for length in lengths:
        vectors.append(small[start : start + length])
        start += length
    down_out = down_full.transpose(1, 2, 0, 3).reshape(hidden, width).astype(f32)
    attn_out = attn_full.transpose(1, 2, 0, 3).reshape(shard, width).astype(f32)
    up_out = up_full.transpose(1, 3, 2, 0, 4).reshape(shard, n * hidden).astype(f32)
    mix_out = (
        mix_full.transpose(1, 3, 2, 0, 4)
        .reshape(shard, n, 3, shard)
        .transpose(0, 2, 1, 3)
        .reshape(shard, 3 * width)
        .astype(f32)
    )
    return (
        block_output.reshape(1, rows, width),
        input_grad.reshape(1, rows, width),
        vectors[0],
        vectors[1],
        mix_out,
        vectors[2],
        vectors[3],
        attn_out,
        vectors[4],
        vectors[5],
        vectors[6],
        up_out,
        vectors[7],
        down_out,
        vectors[8],
    )


def fits(mesh):
    n, ctx = mesh.shape["dp"], mesh.shape["ctx"]
    return H % n == 0 and ctx == 2 * n and n & (n - 1) == 0


def solution(mesh):
    placed = (
        P("dp", "ctx", None),
        P("dp", "ctx", None),
        P(),
        P(),
        P("dp", None),
        P(),
        P(),
        P("dp", None),
        P(),
        P(),
        P(),
        P("dp", None),
        P(),
        P("dp", None),
        P(),
    )
    return jax.shard_map(
        tensor_body if fits(mesh) else body,
        mesh=mesh,
        in_specs=placed,
        out_specs=(
            P("dp", "ctx", None),
            P("dp", "ctx", None),
            P(),
            P(),
            P("dp", None),
            P(),
            P(),
            P("dp", None),
            P(),
            P(),
            P(),
            P("dp", None),
            P(),
            P("dp", None),
            P(),
        ),
        check_vma=False,
    )
```

```python
import functools
import math

import jax
import jax.numpy as jnp
from jax import lax
from jax.experimental import pallas as pl
from jax.experimental.pallas import tpu as pltpu
from jax.sharding import PartitionSpec as P

H = 12
HD = 64


EPS = 1e-05
GELU_C = math.sqrt(2.0 / math.pi)


def from_behind(value, axis, steps):
    count = lax.axis_size(axis)
    pairs = [(source, (source + steps) % count) for source in range(count)]
    return lax.ppermute(value, axis, pairs)


def layer_norm(x, gain, shift):
    centered = x - jnp.mean(x, axis=-1, keepdims=True)
    rstd = lax.rsqrt(jnp.mean(centered * centered, axis=-1, keepdims=True) + EPS)
    x_hat = centered * rstd
    return (x_hat, rstd, x_hat * gain + shift)


def norm_back(grad, x_hat, rstd, gain):
    g = grad * gain
    return rstd * (
        g
        - jnp.mean(g, axis=-1, keepdims=True)
        - x_hat * jnp.mean(g * x_hat, axis=-1, keepdims=True)
    )


def gelu_pair(u):
    inner = GELU_C * (u + 0.044715 * u * u * u)
    t = jnp.tanh(inner)
    value = 0.5 * u * (1.0 + t)
    slope = 0.5 * (1.0 + t) + 0.5 * u * (1.0 - t * t) * GELU_C * (1.0 + 3.0 * 0.044715 * u * u)
    return (value, slope)


def matmul(a, b):
    return jnp.dot(a, b, preferred_element_type=jnp.float32)


def matmul_tn(a, b):
    return lax.dot_general(a, b, (((0,), (0,)), ((), ())), preferred_element_type=jnp.float32)


def matmul_nt(a, b):
    return lax.dot_general(a, b, (((1,), (1,)), ((), ())), preferred_element_type=jnp.float32)


def body(
    block_input,
    out_cotangent,
    first_gain,
    first_shift,
    mix_weight,
    query_bias,
    value_bias,
    attn_weight,
    attn_bias,
    second_gain,
    second_shift,
    up_weight,
    up_bias,
    down_weight,
    down_bias,
):
    rows = block_input.shape[1]
    width = block_input.shape[2]
    scale = HD ** (-0.5)
    x_rows = block_input.reshape(rows, width)
    cot = out_cotangent.reshape(rows, width)
    mix_full, attn_full, up_full, down_full = (
        lax.all_gather(mix_weight, "dp", axis=0, tiled=True),
        lax.all_gather(attn_weight, "dp", axis=0, tiled=True),
        lax.all_gather(up_weight, "dp", axis=0, tiled=True),
        lax.all_gather(down_weight, "dp", axis=0, tiled=True),
    )
    first_hat, first_rstd, first_out = layer_norm(x_rows, first_gain, first_shift)
    first_in = first_out.astype(jnp.bfloat16)
    mixed = matmul(first_in, mix_full)
    queries = (mixed[:, :width] + query_bias).astype(jnp.bfloat16)
    keys = mixed[:, width : 2 * width].astype(jnp.bfloat16)
    values = (mixed[:, 2 * width :] + value_bias).astype(jnp.bfloat16)
    q3 = queries.reshape(rows, H, HD)
    me = lax.axis_index("ctx")
    cycle_size = lax.axis_size("ctx")
    q_pos = me * rows + jnp.arange(rows)
    q_last = me * rows + rows - 1
    start_state = (
        jnp.full((H, rows), -1e30, jnp.float32),
        jnp.zeros((H, rows), jnp.float32),
        jnp.zeros((H, rows, HD), jnp.float32),
    )
    carry = start_state
    key_piece = lax.all_gather(keys, "ctx", axis=0, tiled=True)
    value_piece = lax.all_gather(values, "ctx", axis=0, tiled=True)
    count = key_piece.shape[0]
    kblock = math.gcd(count, 512)
    nblocks = count // kblock
    key_blocks = key_piece.reshape(nblocks, kblock, H, HD)
    value_blocks = value_piece.reshape(nblocks, kblock, H, HD)
    offsets = jnp.arange(nblocks) * kblock

    def one_block(state, item):
        key_blk, value_blk, offset = item

        def compute(state_in):
            run_max, run_total, run_acc = state_in
            key_pos = offset + jnp.arange(kblock)
            allowed = (key_pos[None, :] <= q_pos[:, None])[None]
            scores = (
                jnp.einsum("qhd,khd->hqk", q3, key_blk, preferred_element_type=jnp.float32) * scale
            )
            scores = jnp.where(allowed, scores, -1e30)
            new_max = jnp.maximum(run_max, jnp.max(scores, axis=-1))
            expo = jnp.where(allowed, jnp.exp(scores - new_max[..., None]), 0.0)
            factor = jnp.exp(run_max - new_max)
            new_total = run_total * factor + jnp.sum(expo, axis=-1)
            new_acc = run_acc * factor[..., None] + jnp.einsum(
                "hqk,khd->hqd", expo, value_blk.astype(jnp.float32), precision=lax.Precision.HIGHEST
            )
            return (new_max, new_total, new_acc)

        def keep_state(state_in):
            return state_in

        return (lax.cond(offset <= q_last, compute, keep_state, state), None)

    carry, unused = lax.scan(one_block, carry, (key_blocks, value_blocks, offsets))
    run_max, run_total, run_acc = carry
    attended = (
        (run_acc / run_total[..., None])
        .transpose(1, 0, 2)
        .reshape(rows, width)
        .astype(jnp.bfloat16)
    )
    lse = run_max + jnp.log(run_total)
    after_attn = x_rows + matmul(attended, attn_full) + attn_bias
    second_hat, second_rstd, second_out = layer_norm(after_attn, second_gain, second_shift)
    second_in = second_out.astype(jnp.bfloat16)
    pre_act = matmul(second_in, up_full) + up_bias
    act_value, act_slope = gelu_pair(pre_act)
    activ = act_value.astype(jnp.bfloat16)
    block_output = after_attn + matmul(activ, down_full) + down_bias
    mix_back, attn_back, up_back, down_back = (
        lax.all_gather(mix_weight, "dp", axis=0, tiled=True),
        lax.all_gather(attn_weight, "dp", axis=0, tiled=True),
        lax.all_gather(up_weight, "dp", axis=0, tiled=True),
        lax.all_gather(down_weight, "dp", axis=0, tiled=True),
    )
    cot_b = cot.astype(jnp.bfloat16)
    down_weight_grad = matmul_tn(activ, cot_b)
    down_bias_grad = jnp.sum(cot, axis=0)
    pre_grad = matmul_nt(cot_b, down_back) * act_slope
    pre_grad_b = pre_grad.astype(jnp.bfloat16)
    up_weight_grad = matmul_tn(second_in, pre_grad_b)
    up_bias_grad = jnp.sum(pre_grad, axis=0)
    second_grad = matmul_nt(pre_grad_b, up_back)
    second_gain_grad = jnp.sum(second_grad * second_hat, axis=0)
    second_shift_grad = jnp.sum(second_grad, axis=0)
    resid_grad = cot + norm_back(second_grad, second_hat, second_rstd, second_gain)
    resid_b = resid_grad.astype(jnp.bfloat16)
    attn_weight_grad = matmul_tn(attended, resid_b)
    attn_bias_grad = jnp.sum(resid_grad, axis=0)
    attended_grad = matmul_nt(resid_b, attn_back).astype(jnp.bfloat16)
    grad3 = attended_grad.reshape(rows, H, HD)
    delta = jnp.sum(
        grad3.astype(jnp.float32) * attended.astype(jnp.float32).reshape(rows, H, HD), axis=-1
    ).T

    def block_grads(key_blk, value_blk, key_start):
        count = key_blk.shape[0]
        key3 = key_blk.reshape(count, H, HD)
        value3 = value_blk.reshape(count, H, HD)
        key_pos = key_start + jnp.arange(count)
        allowed = (key_pos[None, :] <= q_pos[:, None])[None]
        scores = jnp.einsum("qhd,khd->hqk", q3, key3, preferred_element_type=jnp.float32) * scale
        probs = jnp.where(allowed, jnp.exp(scores - lse[..., None]), 0.0)
        dprob = jnp.einsum("qhd,khd->hqk", grad3, value3, preferred_element_type=jnp.float32)
        dscore = probs * (dprob - delta[..., None])
        probs_b = probs.astype(jnp.bfloat16)
        dscore_b = dscore.astype(jnp.bfloat16)
        value_add = jnp.einsum("hqk,qhd->khd", probs_b, grad3, preferred_element_type=jnp.float32)
        key_add = (
            jnp.einsum("hqk,qhd->khd", dscore_b, q3, preferred_element_type=jnp.float32) * scale
        )
        query_add = (
            jnp.einsum("hqk,khd->qhd", dscore_b, key3, preferred_element_type=jnp.float32) * scale
        )
        return (
            query_add.reshape(rows, width),
            key_add.reshape(count, width),
            value_add.reshape(count, width),
        )

    def skip_grads(key_blk, value_blk, key_start):
        count = key_blk.shape[0]
        empty = jnp.zeros((count, width), jnp.float32)
        return (jnp.zeros((rows, width), jnp.float32), empty, empty)

    zeros = jnp.zeros((rows, width), jnp.float32)

    def pass_grads(key_acc, value_acc):
        return (
            from_behind(key_acc.astype(jnp.bfloat16), "ctx", -1).astype(key_acc.dtype),
            from_behind(value_acc.astype(jnp.bfloat16), "ctx", -1).astype(value_acc.dtype),
        )

    def cycle_turn(step, state):
        key_blk, value_blk, key_acc, value_acc, query_acc = state
        owner = (me + step) % cycle_size
        query_add, key_add, value_add = lax.cond(
            owner <= me, block_grads, skip_grads, key_blk, value_blk, owner * rows
        )
        key_blk, value_blk = from_behind((key_blk, value_blk), "ctx", -1)
        key_acc, value_acc = pass_grads(key_acc + key_add, value_acc + value_add)
        return (key_blk, value_blk, key_acc, value_acc, query_acc + query_add)

    key_blk, value_blk, key_acc, value_acc, query_acc = lax.fori_loop(
        0, cycle_size - 1, cycle_turn, (keys, values, zeros, zeros, zeros)
    )
    last_owner = (me + cycle_size - 1) % cycle_size
    query_add, key_add, value_add = lax.cond(
        last_owner <= me, block_grads, skip_grads, key_blk, value_blk, last_owner * rows
    )
    key_grad, value_grad = pass_grads(key_acc + key_add, value_acc + value_add)
    query_grad = query_acc + query_add
    query_bias_grad = jnp.sum(query_grad, axis=0)
    value_bias_grad = jnp.sum(value_grad, axis=0)
    mixed_grad = jnp.concatenate([query_grad, key_grad, value_grad], axis=1).astype(jnp.bfloat16)
    mix_weight_grad = matmul_tn(first_in, mixed_grad)
    first_grad = matmul_nt(mixed_grad, mix_back)
    first_gain_grad = jnp.sum(first_grad * first_hat, axis=0)
    first_shift_grad = jnp.sum(first_grad, axis=0)
    input_grad = resid_grad + norm_back(first_grad, first_hat, first_rstd, first_gain)
    local_mats = (mix_weight_grad, attn_weight_grad, up_weight_grad, down_weight_grad)
    shard_sums = (
        lax.psum_scatter(
            local_mats[0].astype(jnp.bfloat16), "dp", scatter_dimension=0, tiled=True
        ).astype(jnp.float32),
        lax.psum_scatter(
            local_mats[1].astype(jnp.bfloat16), "dp", scatter_dimension=0, tiled=True
        ).astype(jnp.float32),
        lax.psum_scatter(
            local_mats[2].astype(jnp.bfloat16), "dp", scatter_dimension=0, tiled=True
        ).astype(jnp.float32),
        lax.psum_scatter(
            local_mats[3].astype(jnp.bfloat16), "dp", scatter_dimension=0, tiled=True
        ).astype(jnp.float32),
    )
    mats = (
        lax.psum(shard_sums[0].astype(jnp.bfloat16), "ctx").astype(jnp.float32),
        lax.psum(shard_sums[1].astype(jnp.bfloat16), "ctx").astype(jnp.float32),
        lax.psum(shard_sums[2].astype(jnp.bfloat16), "ctx").astype(jnp.float32),
        lax.psum(shard_sums[3].astype(jnp.bfloat16), "ctx").astype(jnp.float32),
    )
    smalls = lax.psum(
        (
            first_gain_grad,
            first_shift_grad,
            query_bias_grad,
            value_bias_grad,
            attn_bias_grad,
            second_gain_grad,
            second_shift_grad,
            up_bias_grad,
            down_bias_grad,
        ),
        ("dp", "ctx"),
    )
    return (
        block_output.reshape(1, rows, width),
        input_grad.reshape(1, rows, width),
        smalls[0],
        smalls[1],
        mats[0],
        smalls[2],
        smalls[3],
        mats[1],
        smalls[4],
        smalls[5],
        smalls[6],
        mats[2],
        smalls[7],
        mats[3],
        smalls[8],
    )


def flip(index, mask):
    bit = 1
    while bit <= mask:
        if mask & bit:
            index = index + bit - 2 * bit * ((index // bit) % 2)
        bit *= 2
    return index


def group_size(group, sizes):
    return {"dp": sizes[0], "z": sizes[1] // 2, "core": 2}[group]


def exchange_kernel(plan, sizes, *refs):
    count = len(plan)
    ins, outs = refs[:count], refs[count : 2 * count]
    send_sem, recv_sem, local_sem = refs[2 * count :]
    dp, ctx = lax.axis_index("dp"), lax.axis_index("ctx")
    slots = {"dp": dp, "z": ctx // 2, "core": ctx % 2}

    def peer(group, step):
        if group == "dp":
            return (flip(dp, step), ctx)
        return (dp, flip(ctx, 2 * step if group == "z" else step))

    barrier = pltpu.get_barrier_semaphore()
    greeted = 0
    for group in sorted({group for group, mode in plan}):
        for step in range(1, group_size(group, sizes)):
            pl.semaphore_signal(
                barrier, inc=1, device_id=peer(group, step), device_id_type=pl.DeviceIdType.MESH
            )
            greeted += 1
    pl.semaphore_wait(barrier, greeted)
    copies = []
    for item, (group, mode) in enumerate(plan):
        me = slots[group]
        for step in range(group_size(group, sizes) - 1, -1, -1):
            pieces = piece_refs(ins[item], outs[item], mode, me, flip(me, step))
            for part, (source, target) in enumerate(pieces):
                number = step * PARTS + part
                if step == 0:
                    copy = pltpu.make_async_copy(source, target, local_sem.at[item, part])
                else:
                    copy = pltpu.make_async_remote_copy(
                        src_ref=source,
                        dst_ref=target,
                        send_sem=send_sem.at[item, number],
                        recv_sem=recv_sem.at[item, number],
                        device_id=peer(group, step),
                        device_id_type=pl.DeviceIdType.MESH,
                    )
                copy.start()
                copies.append(copy)
    for copy in copies:
        copy.wait()


PARTS = 4


def piece_refs(source, target, mode, me, other):
    if mode == "a2a":
        return [(source.at[other], target.at[me])]
    if mode == "cols":
        size = target.shape[2]
        return [(source.at[:, pl.ds(pl.multiple_of(other * size, 128), size)], target.at[me])]
    if mode == "lanes":
        parts, size = source.shape[1], source.shape[3]
        step = target.shape[2] // parts
        return [
            (
                source.at[:, part],
                target.at[:, :, pl.ds(pl.multiple_of(part * step + me * size, 128), size)],
            )
            for part in range(parts)
        ]
    return [(source, target.at[me])]


def exchange_shape(shape, mode, n):
    if mode == "a2a":
        return shape
    if mode == "cols":
        return (n, shape[0], shape[1] // n)
    if mode == "lanes":
        return (shape[0], shape[2], shape[1] * n * shape[3])
    return (n,) + shape


def exchange(number, *items):
    sizes = (lax.axis_size("dp"), lax.axis_size("ctx"))
    plan = tuple((group, mode) for group, mode, value in items)
    values = [value for group, mode, value in items]
    shapes = [
        jax.ShapeDtypeStruct(
            exchange_shape(value.shape, mode, group_size(group, sizes)), value.dtype
        )
        for group, mode, value in items
    ]
    most = PARTS * max(group_size(group, sizes) for group, mode in plan)
    return pl.pallas_call(
        functools.partial(exchange_kernel, plan, sizes),
        out_shape=shapes,
        in_specs=[pl.BlockSpec(memory_space=pltpu.VMEM)] * len(values),
        out_specs=[pl.BlockSpec(memory_space=pl.ANY)] * len(values),
        scratch_shapes=[
            pltpu.SemaphoreType.DMA((len(values), most)),
            pltpu.SemaphoreType.DMA((len(values), most)),
            pltpu.SemaphoreType.DMA((len(values), PARTS)),
        ],
        compiler_params=pltpu.CompilerParams(collective_id=number, has_side_effects=True),
        name="exchange_%d" % number,
    )(*values)


def head_columns(ref, part, head, heads):
    start = (part * heads + head) * HD
    return ref[:, start : start + HD]


def attend_kernel(scale, heads, mixed_ref, kv_ref, qpos_ref, kpos_ref, out_ref, lse_ref):
    allowed = kpos_ref[...] <= qpos_ref[...]
    for head in range(heads):
        q = head_columns(mixed_ref, 0, head, heads)
        k = head_columns(kv_ref, 0, head, heads)
        v = head_columns(kv_ref, 1, head, heads)
        scores = jnp.where(allowed, matmul_nt(q, k) * scale, -1e30)
        top = jnp.max(scores, axis=-1, keepdims=True)
        weights = jnp.exp(scores - top)
        total = jnp.sum(weights, axis=-1, keepdims=True)
        result = matmul(weights.astype(jnp.bfloat16), v) / total
        out_ref[:, head * HD : (head + 1) * HD] = result.astype(jnp.bfloat16)
        lse_ref[:, head : head + 1] = top + jnp.log(total)


def attend_back_kernel(
    scale, heads, mixed_ref, kv_ref, qpos_ref, kpos_ref, out_ref, lse_ref, grad_ref,
    dq_ref, dkv_ref, qsum_ref, vsum_ref,
):
    allowed = kpos_ref[...] <= qpos_ref[...]
    for head in range(heads):
        q = head_columns(mixed_ref, 0, head, heads)
        k = head_columns(kv_ref, 0, head, heads)
        v = head_columns(kv_ref, 1, head, heads)
        grad = head_columns(grad_ref, 0, head, heads)
        out = head_columns(out_ref, 0, head, heads)
        delta = jnp.sum(
            grad.astype(jnp.float32) * out.astype(jnp.float32), axis=-1, keepdims=True
        )
        lse = lse_ref[:, head : head + 1]
        probs = jnp.where(allowed, jnp.exp(matmul_nt(q, k) * scale - lse), 0.0)
        dscore = (probs * (matmul_nt(grad, v) - delta)).astype(jnp.bfloat16)
        dv = matmul_tn(probs.astype(jnp.bfloat16), grad)
        dk = matmul_tn(dscore, q) * scale
        dq = matmul(dscore, k) * scale
        first, last = head * HD, (head + 1) * HD
        dq_ref[:, first:last] = dq.astype(jnp.bfloat16)
        dkv_ref[:, first:last] = dk.astype(jnp.bfloat16)
        dkv_ref[:, heads * HD + first : heads * HD + last] = dv.astype(jnp.bfloat16)
        qsum_ref[:, first:last] = jnp.sum(dq, axis=0, keepdims=True)
        vsum_ref[:, first:last] = jnp.sum(dv, axis=0, keepdims=True)


def local_call(kernel, name, values, outs):
    return pl.pallas_call(
        kernel,
        out_shape=[jax.ShapeDtypeStruct(shape, dtype) for shape, dtype in outs],
        in_specs=[pl.BlockSpec(memory_space=pltpu.VMEM)] * len(values),
        out_specs=[pl.BlockSpec(memory_space=pltpu.VMEM)] * len(outs),
        name=name,
    )(*values)


def tensor_body(
    block_input,
    out_cotangent,
    first_gain,
    first_shift,
    mix_weight,
    query_bias,
    value_bias,
    attn_weight,
    attn_bias,
    second_gain,
    second_shift,
    up_weight,
    up_bias,
    down_weight,
    down_bias,
):
    b16, f32 = jnp.bfloat16, jnp.float32
    n, nz = lax.axis_size("dp"), lax.axis_size("ctx") // 2
    rows, width = block_input.shape[1:]
    total_rows = n * rows
    shard = width // n
    heads = H // n
    hidden = up_weight.shape[1] // n
    scale = HD ** (-0.5)
    dp, core = lax.axis_index("dp"), lax.axis_index("ctx") % 2
    x_rows = block_input.reshape(rows, width)
    cot = out_cotangent.reshape(rows, width)
    cot_b = cot.astype(b16)

    def total(value):
        return jnp.sum(value.astype(f32), axis=0)

    first_hat, first_rstd, first_out = layer_norm(x_rows, first_gain, first_shift)
    mix_parts = mix_weight.reshape(shard, 3, n, shard).transpose(2, 0, 1, 3).reshape(n, shard, 3 * shard)
    mix_cols, first_all = exchange(
        0, ("dp", "a2a", mix_parts), ("dp", "ag", first_out.astype(b16))
    )
    mix_cols = mix_cols.reshape(width, 3 * shard)
    first_all = first_all.reshape(total_rows, width)
    own = lambda vector, size: lax.dynamic_slice(vector, (dp * size,), (size,))
    mix_bias = jnp.concatenate(
        [own(query_bias, shard), jnp.zeros((shard,), f32), own(value_bias, shard)]
    )
    mixed = (matmul(first_all, mix_cols) + mix_bias).astype(b16)
    mixed_seq, up_cols = exchange(
        1, ("z", "a2a", mixed.reshape(n, rows, 3 * shard)), ("dp", "cols", up_weight)
    )
    up_cols = up_cols.reshape(width, hidden)
    (kv_seq,) = exchange(2, ("core", "ag", mixed_seq[:, :, shard:]))

    q_rows, k_rows = nz * rows, 2 * nz * rows
    kv_flat = kv_seq.reshape(k_rows, 2 * shard)
    mixed_flat = mixed_seq.reshape(q_rows, 3 * shard)
    q_idx, k_idx = jnp.arange(q_rows), jnp.arange(k_rows)
    q_pos = ((q_idx // rows) * 2 + core) * rows + q_idx % rows
    k_pos = (((k_idx % q_rows) // rows) * 2 + k_idx // q_rows) * rows + k_idx % rows
    shared = (q_pos.astype(jnp.int32)[:, None], k_pos.astype(jnp.int32)[None, :])
    out_seq, lse = local_call(
        functools.partial(attend_kernel, scale, heads),
        "attend",
        (mixed_flat, kv_flat) + shared,
        (((q_rows, shard), b16), ((q_rows, heads), f32)),
    )
    attended, cot_all = exchange(
        3, ("z", "a2a", out_seq.reshape(nz, rows, shard)), ("dp", "ag", cot_b)
    )
    cot_all = cot_all.reshape(total_rows, width)
    attended = attended.reshape(total_rows, shard)
    (attn_parts,) = exchange(
        4, ("dp", "a2a", matmul(attended, attn_weight).astype(b16).reshape(n, rows, width))
    )
    after_attn = x_rows + total(attn_parts) + attn_bias
    second_hat, second_rstd, second_out = layer_norm(after_attn, second_gain, second_shift)
    (second_all,) = exchange(5, ("dp", "ag", second_out.astype(b16)))
    second_all = second_all.reshape(total_rows, width)
    pre_act = matmul(second_all, up_cols) + own(up_bias, hidden)
    act_value, act_slope = gelu_pair(pre_act)
    activ = act_value.astype(b16)
    out_part = matmul(activ, down_weight).astype(b16)
    pre_grad = matmul_nt(cot_all, down_weight) * act_slope
    pre_grad_b = pre_grad.astype(b16)
    second_part = matmul_nt(pre_grad_b, up_cols).astype(b16)
    down_grad = matmul_tn(activ, cot_all).astype(b16)
    up_grad = matmul_tn(second_all, pre_grad_b).astype(b16)
    up_bias_grad = jnp.sum(pre_grad, axis=0)

    def halves(value):
        return value.reshape(value.shape[0], 2, -1).transpose(1, 0, 2)

    def by_rows(value):
        columns = value.shape[-1]
        return value.reshape(n, nz, shard // nz, columns).transpose(1, 0, 2, 3)

    down_pair, up_pair = exchange(16, ("core", "cols", down_grad), ("core", "cols", up_grad))
    down_sum = total(down_pair).astype(b16).reshape(nz, hidden // nz, width // 2)
    up_sum = by_rows(total(up_pair).astype(b16))
    out_parts, second_parts, down_z = exchange(
        6,
        ("dp", "a2a", out_part.reshape(n, rows, width)),
        ("dp", "a2a", second_part.reshape(n, rows, width)),
        ("z", "a2a", down_sum),
    )
    block_output = after_attn + total(out_parts) + down_bias
    second_grad = total(second_parts)
    resid_grad = cot + norm_back(second_grad, second_hat, second_rstd, second_gain)
    resid_all, up_z = exchange(
        7,
        ("dp", "ag", resid_grad.astype(b16)),
        ("z", "a2a", up_sum),
    )
    resid_all = resid_all.reshape(total_rows, width)
    attended_grad = matmul_nt(resid_all, attn_weight).astype(b16)
    attn_grad = matmul_tn(attended, resid_all).astype(b16)
    down_piece = total(down_z).astype(b16)
    up_piece = total(up_z).astype(b16)
    grad_seq, up_dp, attn_pair = exchange(
        8,
        ("z", "a2a", attended_grad.reshape(n, rows, shard)),
        ("dp", "a2a", up_piece),
        ("core", "cols", attn_grad),
    )
    query_grad, key_value, query_sum, value_sum = local_call(
        functools.partial(attend_back_kernel, scale, heads),
        "attend_back",
        (mixed_flat, kv_flat) + shared + (out_seq, lse, grad_seq.reshape(q_rows, shard)),
        (
            ((q_rows, shard), b16),
            ((k_rows, 2 * shard), b16),
            ((1, shard), f32),
            ((1, shard), f32),
        ),
    )
    query_sum, value_sum = query_sum.reshape(shard), value_sum.reshape(shard)
    (kv_pair,) = exchange(9, ("core", "a2a", key_value.reshape(2, nz, rows, 2 * shard)))
    mixed_back = jnp.concatenate(
        [query_grad.reshape(nz, rows, shard), total(kv_pair).astype(b16)], axis=-1
    )
    attn_sum = total(attn_pair).astype(b16).reshape(nz, shard // nz, width // 2)
    mixed_grad, attn_z = exchange(10, ("z", "a2a", mixed_back), ("z", "a2a", attn_sum))
    mixed_grad = mixed_grad.reshape(total_rows, 3 * shard)
    first_part = matmul_nt(mixed_grad, mix_cols).astype(b16)
    mix_grad = matmul_tn(first_all, mixed_grad).astype(b16)
    attn_piece = total(attn_z).astype(b16)
    first_parts, mix_pair, up_all, attn_all = exchange(
        11,
        ("dp", "a2a", first_part.reshape(n, rows, width)),
        ("core", "a2a", halves(mix_grad)),
        ("z", "ag", up_dp),
        ("z", "ag", attn_piece),
    )
    first_grad = total(first_parts)
    input_grad = resid_grad + norm_back(first_grad, first_hat, first_rstd, first_gain)

    def spread(vector, full):
        return lax.dynamic_update_slice(
            jnp.zeros((full,), f32), vector, (dp * vector.shape[0],)
        )

    smalls = [
        jnp.sum(first_grad * first_hat, axis=0),
        jnp.sum(first_grad, axis=0),
        spread(query_sum, width),
        spread(value_sum, width),
        jnp.sum(resid_grad, axis=0),
        jnp.sum(second_grad * second_hat, axis=0),
        jnp.sum(second_grad, axis=0),
        spread(up_bias_grad, hidden * n),
        jnp.sum(cot, axis=0),
    ]
    lengths = [vector.shape[0] for vector in smalls]
    small = jnp.concatenate(smalls).reshape(-1, 128)
    mix_sum = by_rows(total(mix_pair).astype(b16))
    mix_z, small_pair, up_full, attn_full = exchange(
        12,
        ("z", "a2a", mix_sum),
        ("core", "ag", small),
        ("core", "lanes", up_all),
        ("core", "lanes", attn_all[:, None]),
    )
    mix_dp, small_z, down_all = exchange(
        13,
        ("dp", "a2a", total(mix_z).astype(b16)),
        ("z", "ag", total(small_pair)),
        ("z", "ag", down_piece),
    )
    mix_all, small_dp, down_full = exchange(
        14,
        ("z", "ag", mix_dp),
        ("dp", "ag", total(small_z)),
        ("core", "lanes", down_all[:, None]),
    )
    (mix_full,) = exchange(15, ("core", "ag", mix_all))
    small = total(small_dp).reshape(-1)
    vectors, start = [], 0
    for length in lengths:
        vectors.append(small[start : start + length])
        start += length
    down_out = down_full.reshape(hidden, width).astype(f32)
    attn_out = attn_full.reshape(shard, width).astype(f32)
    up_out = up_full.reshape(shard, n * hidden).astype(f32)
    mix_out = (
        mix_full.transpose(1, 3, 2, 0, 4)
        .reshape(shard, n, 3, shard)
        .transpose(0, 2, 1, 3)
        .reshape(shard, 3 * width)
        .astype(f32)
    )
    return (
        block_output.reshape(1, rows, width),
        input_grad.reshape(1, rows, width),
        vectors[0],
        vectors[1],
        mix_out,
        vectors[2],
        vectors[3],
        attn_out,
        vectors[4],
        vectors[5],
        vectors[6],
        up_out,
        vectors[7],
        down_out,
        vectors[8],
    )


def fits(mesh):
    n, ctx = mesh.shape["dp"], mesh.shape["ctx"]
    return H % n == 0 and ctx == 2 * n and n == PARTS


def solution(mesh):
    placed = (
        P("dp", "ctx", None),
        P("dp", "ctx", None),
        P(),
        P(),
        P("dp", None),
        P(),
        P(),
        P("dp", None),
        P(),
        P(),
        P(),
        P("dp", None),
        P(),
        P("dp", None),
        P(),
    )
    return jax.shard_map(
        tensor_body if fits(mesh) else body,
        mesh=mesh,
        in_specs=placed,
        out_specs=(
            P("dp", "ctx", None),
            P("dp", "ctx", None),
            P(),
            P(),
            P("dp", None),
            P(),
            P(),
            P("dp", None),
            P(),
            P(),
            P(),
            P("dp", None),
            P(),
            P("dp", None),
            P(),
        ),
        check_vma=False,
    )
```
